768 devices in a mesh: block: 48 (over y, z_lo), chan: 16 (over x, z_hi, core).
Axes of the slice: x: 4, y: 8, z: 12 (z_hi: 2, z_lo: 6; z = z_hi * 6 + z_lo), core: 2. Of those that a mesh axis runs over, the one named last changes fastest.
Arguments:
- volume: bfloat16 [16, 192, 64, 128], P(None, 'block', 'chan'), may hold values from -6 to 6
- kernel: bfloat16 [32, 27, 16], replicated, may hold values from -0.3125 to 0.3125
- conv_bias: float32 [32], replicated, may hold values from -0.5 to 0.5
- pooled_grad: bfloat16 [32, 96, 32, 64], P(None, 'block', 'chan'), may hold values from -40 to 40
Outputs:
- pooled: bfloat16 [32, 96, 32, 64], P(None, 'block', 'chan')
- volume_grad: bfloat16 [16, 192, 64, 128], P(None, 'block', 'chan')
- kernel_grad: float32 [32, 27, 16], replicated
- bias_grad: float32 [32], replicated
The draws below stay inside these ranges and needn't reach their ends.
All inputs are finite; a program needn't handle non-finite values.
Results may differ from the reference program's by a relative error of at most 0.005.
Values may be sent and summed in bfloat16 or wider, within the bound.
A program may use at most 32 MiB of HBM per device.

```python
import math
import jax
import jax.numpy as jnp
from jax import lax

CIN = 16
COUT = 32
CX = 4
NZ = 128
NX = 192
NY = 64


def draw_pooled_grad(key, part):
    key_base = jax.random.fold_in(key, 11)
    key_level = jax.random.fold_in(key, 12)
    row_total = NX // 2
    shape_full = (COUT, row_total, NY // 2, NZ // 2)
    level = jax.random.uniform(key_level, (1, row_total, 1, 1), jnp.float32)
    ramp = 1.0 + 2.0 * jnp.arange(row_total, dtype=jnp.float32).reshape(1, row_total, 1, 1) / max(row_total - 1, 1)
    factor = ramp * jnp.exp(level * math.log(10.0))
    base = jax.random.normal(key_base, shape_full, jnp.float32)
    return jnp.clip(base * factor, -40.0, 40.0).astype(jnp.bfloat16)


def level_of(stream_key, shape, cuts, least, largest):
    def one(dim, shards_of):
        steps = jax.random.uniform(jax.random.fold_in(jax.random.fold_in(stream_key, 6), dim), (shards_of,), jnp.float32, least / len(cuts), largest / len(cuts))
        return jnp.repeat(jnp.exp(steps), shape[dim] // shards_of).reshape((-1,) + (1,) * (len(shape) - dim - 1))

    factor_of = one(*cuts[0])
    for cut in cuts[1:]:
        factor_of = factor_of * one(*cut)
    return factor_of


def scatter_about(key, dims, width, bound, cuts=(), kind=jnp.bfloat16):
    drawn = jax.random.normal(key, dims, jnp.float32) * width
    if len(cuts) > 0:
        drawn = level_of(key, dims, cuts, -0.22, 0.18) * drawn
    return jnp.clip(drawn, min=-bound, max=bound).astype(kind)


def setup_inputs(seed: int = 0) -> dict:
    key_of = jax.random.split(jax.random.key(seed), 5)
    volume = scatter_about(key_of[0], (CIN, NX, NY, NZ), 1.0, 6.0, ((1, 48), (2, 16)))
    kernel = scatter_about(key_of[1], (COUT, 27, CIN), (27 * CIN) ** -0.5, 0.3125)
    conv_bias = jnp.clip(jax.random.uniform(key_of[2], (COUT,), jnp.float32, -0.5, 0.5), -0.5, 0.5)
    pooled_grad = draw_pooled_grad(jax.random.fold_in(key_of[4], 71), 0)
    return dict(volume=volume, kernel=kernel, conv_bias=conv_bias, pooled_grad=pooled_grad)


def conv_rows(inputs, filters):
    return lax.conv_general_dilated(inputs[None], filters, (1, 1, 1), ((0, 0), (1, 1), (1, 1)), dimension_numbers=("NCDHW", "OIDHW", "NCDHW"), precision=lax.Precision.HIGHEST)[0]


def reference(volume, kernel, conv_bias, pooled_grad):
    weights = kernel.astype(jnp.float32).reshape(COUT, 3, 3, 3, CIN)
    fwd_filters = weights.transpose(0, 4, 1, 2, 3)
    back_filters = weights[:, ::-1, ::-1, ::-1, :].transpose(4, 0, 1, 2, 3)
    padded_in = jnp.pad(volume.astype(jnp.float32), ((0, 0), (2, 2), (0, 0), (0, 0)))
    padded_grad = jnp.pad(pooled_grad.astype(jnp.float32), ((0, 0), (1, 1), (0, 0), (0, 0)))
    block_rows = 2 * CX
    half_rows = CX
    block_count = NX // block_rows

    def one_block(index):
        first = index * block_rows
        window = lax.dynamic_slice_in_dim(padded_in, first, block_rows + 4, 1)
        preact = conv_rows(window, fwd_filters) + conv_bias[:, None, None, None]
        inner = preact[:, 1:-1]
        smooth = 0.2 * inner + 0.8 * jax.nn.softplus(inner)
        pooled = smooth.reshape(COUT, half_rows, 2, NY // 2, 2, NZ // 2, 2).mean(axis=(2, 4, 6)).astype(jnp.bfloat16)
        grad_rows = lax.dynamic_slice_in_dim(padded_grad, index * half_rows, half_rows + 2, 1)
        upsampled = jnp.repeat(jnp.repeat(jnp.repeat(grad_rows, 2, 1), 2, 2), 2, 3)[:, 1:-1]
        row_index = first - 1 + jnp.arange(block_rows + 2)
        inside = ((row_index >= 0) & (row_index < NX)).astype(jnp.float32)[None, :, None, None]
        slope = 0.2 + 0.8 * jax.nn.sigmoid(preact)
        pre_grad = (upsampled * 0.125 * slope * inside).astype(jnp.bfloat16).astype(jnp.float32)
        volume_grad = conv_rows(pre_grad, back_filters).astype(jnp.bfloat16)
        shifted = jnp.pad(window[:, 1:-1], ((0, 0), (0, 0), (1, 1), (1, 1)))
        centre = pre_grad[:, 1:-1]
        terms = []
        for row_off in range(3):
            for col_off in range(3):
                for deep_off in range(3):
                    piece = shifted[:, row_off:row_off + block_rows, col_off:col_off + NY, deep_off:deep_off + NZ]
                    terms.append(jnp.einsum("opqr,cpqr->oc", centre, piece, precision=lax.Precision.HIGHEST))
        kernel_grad = jnp.stack(terms, 1)
        bias_grad = jnp.sum(centre, axis=(1, 2, 3))
        return pooled, volume_grad, kernel_grad, bias_grad

    pooled, volume_grad, kernel_grad, bias_grad = lax.map(one_block, jnp.arange(block_count))
    pooled = pooled.transpose(1, 0, 2, 3, 4).reshape(COUT, NX // 2, NY // 2, NZ // 2)
    volume_grad = volume_grad.transpose(1, 0, 2, 3, 4).reshape(CIN, NX, NY, NZ)
    return pooled, volume_grad, jnp.sum(kernel_grad, axis=0), jnp.sum(bias_grad, axis=0)
```

```python
import functools

import jax
import jax.numpy as jnp
from jax import lax
from jax.experimental import pallas as pl
from jax.experimental.pallas import tpu as pltpu
from jax.sharding import PartitionSpec as P

MESH = pl.DeviceIdType.MESH
F32 = jnp.float32
BF16 = jnp.bfloat16
DIRECTIONS = [(i, j) for i in (-1, 0, 1) for j in (-1, 0, 1) if (i, j) != (0, 0)]


def span_out(step):
    return slice(1, 5) if step == 0 else (slice(4, 5) if step > 0 else slice(1, 2))


def span_in(step):
    return slice(1, 5) if step == 0 else (slice(0, 1) if step > 0 else slice(5, 6))


def nt_dot(a, b):
    return lax.dot_general(a, b, (((1,), (1,)), ((), ())), preferred_element_type=F32)


def kernel(factors, vt, w_fwd, w_back, bias, coarse, pooled_o, vgrad_o, kgrad_o,
           wide, shifted, cols, pre, grad, cols_back, terms, from_one, from_two, from_three, result,
           halo_send, halo_recv, grad_send, grad_recv, one_send, one_recv, two_send, two_recv,
           three_send, three_recv, four_send, four_recv):
    ny, nzl, nx, nzh, ncore = factors
    nblock, nchan = ny * nzl, nx * nzh * ncore
    blk, chn = lax.axis_index("block"), lax.axis_index("chan")
    y, zl = lax.div(blk, nzl), lax.rem(blk, nzl)
    x, zh, core = lax.div(chn, nzh * ncore), lax.rem(lax.div(chn, ncore), nzh), lax.rem(chn, ncore)
    n_one, n_two, n_three = nx * ncore, ny, nzh * nzl
    me_one, me_two, me_three = x * ncore + core, y, zh * nzl + zl

    def dev_one(k):
        return (blk, lax.div(k, ncore) * (nzh * ncore) + zh * ncore + lax.rem(k, ncore))

    def dev_two(k):
        return (k * nzl + zl, chn)

    def dev_three(k):
        return (y * nzl + lax.rem(k, nzl), x * (nzh * ncore) + lax.div(k, nzl) * ncore + core)

    def inside(di, dj):
        ok = (blk + di >= 0) & (blk + di < nblock) & (chn + dj >= 0) & (chn + dj < nchan)
        return ok

    groups = ((n_one, me_one, dev_one), (n_two, me_two, dev_two), (n_three, me_three, dev_three))

    wide[...] = jnp.zeros_like(wide)
    grad[...] = jnp.zeros_like(grad)

    barrier = pltpu.get_barrier_semaphore()
    count = jnp.int32(n_one + n_two + n_three - 3)
    for di, dj in DIRECTIONS:
        ok = inside(di, dj)
        count = count + ok.astype(jnp.int32)

        @pl.when(ok)
        def _(di=di, dj=dj):
            pl.semaphore_signal(barrier, inc=1, device_id=(blk + di, chn + dj), device_id_type=MESH)
    for n, me, dev in groups:
        for k in range(1, n):
            pl.semaphore_signal(barrier, inc=1, device_id=dev(lax.rem(me + k, n)), device_id_type=MESH)
    wide[1:5, 1:5] = vt[...]
    cols[:, :, 432:512, :] = jnp.ones((4, 4, 80, 128), BF16)
    pl.semaphore_wait(barrier, count)

    def halo(buf, send, recv, which):
        di, dj = DIRECTIONS[which]
        return pltpu.make_async_remote_copy(
            src_ref=buf.at[span_out(di), span_out(dj)],
            dst_ref=buf.at[span_in(di), span_in(dj)],
            send_sem=send.at[which], recv_sem=recv.at[which],
            device_id=(blk + di, chn + dj), device_id_type=MESH)

    def halo_start(buf, send, recv):
        for which, (di, dj) in enumerate(DIRECTIONS):
            @pl.when(inside(di, dj))
            def _(which=which):
                halo(buf, send, recv, which).start()

    def halo_recv_wait(buf, send, recv):
        for which, (di, dj) in enumerate(DIRECTIONS):
            @pl.when(inside(-di, -dj))
            def _(which=which):
                halo(buf, send, recv, which).wait_recv()

    def halo_send_wait(buf, send, recv):
        for which, (di, dj) in enumerate(DIRECTIONS):
            @pl.when(inside(di, dj))
            def _(which=which):
                halo(buf, send, recv, which).wait_send()

    def group_copy(stage, k, src, dst, send, recv):
        n, me, dev = groups[stage]
        return pltpu.make_async_remote_copy(
            src_ref=src, dst_ref=dst, send_sem=send.at[k], recv_sem=recv.at[k],
            device_id=dev(lax.rem(me + k, n)), device_id_type=MESH)

    halo_start(wide, halo_send, halo_recv)

    row = lax.broadcasted_iota(jnp.int32, (64, 128), 0)
    lane = lax.broadcasted_iota(jnp.int32, (64, 128), 1)
    up_map = (lax.shift_right_logical(lane, 1) == row).astype(F32).astype(BF16)
    ups = [[jnp.dot(coarse[i, j], up_map, preferred_element_type=F32) * 0.125 for j in range(2)] for i in range(2)]
    row2 = lax.broadcasted_iota(jnp.int32, (128, 256), 0)
    lane2 = lax.broadcasted_iota(jnp.int32, (128, 256), 1)
    shift_map = (row2 == jnp.where(lane2 < 128, lane2 - 1, lane2 - 127)).astype(F32).astype(BF16)

    halo_recv_wait(wide, halo_send, halo_recv)

    for i in range(6):
        moved = jnp.dot(wide[i].reshape(96, 128), shift_map, preferred_element_type=F32).astype(BF16)
        shifted[0, i] = moved[:, :128].reshape(6, 16, 128)
        shifted[1, i] = moved[:, 128:].reshape(6, 16, 128)
    for a in range(3):
        for b in range(3):
            for d in range(3):
                t = 9 * a + 3 * b + d
                source = wide if d == 1 else shifted.at[d // 2]
                cols[:, :, 16 * t:16 * t + 16, :] = source[a:a + 4, b:b + 4]
    kacc = jnp.zeros((32, 512), F32)
    for i in range(4):
        for j in range(4):
            act = jnp.dot(w_fwd[...], cols[i, j], preferred_element_type=F32) + bias[...]
            pre[i, j] = act
            slope = 0.2 + 0.8 * jax.nn.sigmoid(act)
            grad[1 + i, 1 + j] = (ups[i // 2][j // 2] * slope).astype(BF16)
    halo_start(grad, grad_send, grad_recv)
    for i in range(4):
        for j in range(0, 4, 2):
            left = jnp.concatenate([grad[1 + i, 1 + j], grad[1 + i, 2 + j]], axis=1)
            right = jnp.concatenate([cols[i, j], cols[i, j + 1]], axis=1)
            kacc = kacc + nt_dot(left, right)
    for s in range(16):
        r, l = s // 4, s % 4
        terms[s] = kacc[8 * r:8 * r + 8, 128 * l:128 * l + 128]

    per = 16 // n_one
    own = pl.ds(me_one * per, per)
    copies = []

    def send_all(stage, make):
        started = [make(k) for k in range(1, groups[stage][0])]
        for c in started:
            c.start()
        copies.extend(started)
        return started

    def total(buf, n):
        acc = buf[0]
        for k in range(1, n):
            acc = acc + buf[k]
        return acc

    one = send_all(0, lambda k: group_copy(
        0, k, terms.at[pl.ds(lax.rem(me_one + k, n_one) * per, per)], from_one.at[me_one], one_send, one_recv))
    from_one[me_one] = terms[own]

    pool_row = lax.broadcasted_iota(jnp.int32, (128, 64), 0)
    pool_lane = lax.broadcasted_iota(jnp.int32, (128, 64), 1)
    pool_map = jnp.where(lax.shift_right_logical(pool_row, 1) == pool_lane, 0.125, 0.0).astype(F32)
    for i in range(2):
        for j in range(2):
            acc = None
            for p in range(2):
                for q in range(2):
                    v = pre[2 * i + p, 2 * j + q]
                    smooth = 0.2 * v + 0.8 * (jnp.maximum(v, 0.0) + jnp.log1p(jnp.exp(-jnp.abs(v))))
                    acc = smooth if acc is None else acc + smooth
            pooled_o[i, j] = jnp.dot(acc, pool_map, precision=lax.Precision.HIGHEST,
                                     preferred_element_type=F32).astype(BF16)

    for c in one:
        c.wait_recv()
    from_two[me_two] = total(from_one, n_one)
    two = send_all(1, lambda k: group_copy(1, k, from_two.at[me_two], from_two.at[me_two], two_send, two_recv))

    halo_recv_wait(grad, grad_send, grad_recv)
    for a in range(3):
        for b in range(3):
            t = 3 * a + b
            cols_back[:, :, 32 * t:32 * t + 32, :] = grad[a:a + 4, b:b + 4]
    zlane = lax.broadcasted_iota(jnp.int32, (16, 128), 1)

    def back_row(i):
        for j in range(4):
            part = jnp.dot(w_back[...], cols_back[i, j], preferred_element_type=F32)
            before = jnp.where(zlane == 0, 0.0, pltpu.roll(part[:16], 1, 1))
            after = jnp.where(zlane == 127, 0.0, pltpu.roll(part[32:], 127, 1))
            vgrad_o[i, j] = (before + part[16:32] + after).astype(BF16)

    for c in two:
        c.wait_recv()
    from_three[me_three] = total(from_two, n_two)
    three = send_all(2, lambda k: group_copy(2, k, from_three.at[me_three], from_three.at[me_three], three_send, three_recv))
    back_row(0)
    back_row(1)
    for c in three:
        c.wait_recv()
    result[own] = total(from_three, n_three)
    four = send_all(0, lambda k: group_copy(0, k, result.at[own], result.at[own], four_send, four_recv))
    back_row(2)
    back_row(3)
    halo_send_wait(wide, halo_send, halo_recv)
    halo_send_wait(grad, grad_send, grad_recv)
    for c in four:
        c.wait_recv()
    for s in range(16):
        r, l = s // 4, s % 4
        kgrad_o[8 * r:8 * r + 8, 128 * l:128 * l + 128] = result[s]
    for c in copies:
        c.wait_send()


def factors_of(mesh):
    nblock, nchan = mesh.shape["block"], mesh.shape["chan"]
    if (nblock, nchan) == (48, 16):
        return (8, 6, 4, 2, 2)
    return (2, nblock // 2, nchan // 4, 2, 2)


def local(factors, volume, weights, conv_bias, pooled_grad):
    ny, nzl, nx, nzh, ncore = factors
    n_one, n_two, n_three = nx * ncore, ny, nzh * nzl
    per = 16 // n_one
    vt = volume.transpose(1, 2, 0, 3)
    w_fwd = jnp.pad(weights.reshape(32, 432), ((0, 0), (0, 80)))
    w5 = weights.reshape(32, 3, 3, 3, 16)[:, ::-1, ::-1, ::-1, :]
    w_back = w5.transpose(3, 4, 1, 2, 0).reshape(48, 288)
    coarse = pooled_grad.transpose(1, 2, 0, 3)
    vmem = pl.BlockSpec(memory_space=pltpu.VMEM)
    dma = pltpu.SemaphoreType.DMA
    pooled, vgrad, kgrad = pl.pallas_call(
        functools.partial(kernel, factors),
        out_shape=(jax.ShapeDtypeStruct((2, 2, 32, 64), BF16),
                   jax.ShapeDtypeStruct((4, 4, 16, 128), BF16),
                   jax.ShapeDtypeStruct((32, 512), F32)),
        in_specs=[vmem] * 5,
        out_specs=(vmem, vmem, vmem),
        scratch_shapes=[
            pltpu.VMEM((6, 6, 16, 128), BF16),
            pltpu.VMEM((2, 6, 6, 16, 128), BF16),
            pltpu.VMEM((4, 4, 512, 128), BF16),
            pltpu.VMEM((4, 4, 32, 128), F32),
            pltpu.VMEM((6, 6, 32, 128), BF16),
            pltpu.VMEM((4, 4, 288, 128), BF16),
            pltpu.VMEM((16, 8, 128), F32),
            pltpu.VMEM((n_one, per, 8, 128), F32),
            pltpu.VMEM((n_two, per, 8, 128), F32),
            pltpu.VMEM((n_three, per, 8, 128), F32),
            pltpu.VMEM((16, 8, 128), F32),
            dma((8,)), dma((8,)), dma((8,)), dma((8,)),
            dma((n_one,)), dma((n_one,)), dma((n_two,)), dma((n_two,)),
            dma((n_three,)), dma((n_three,)), dma((n_one,)), dma((n_one,)),
        ],
        compiler_params=pltpu.CompilerParams(
            collective_id=0, has_side_effects=True, vmem_limit_bytes=32 * 1024 * 1024),
        name="conv_step",
    )(vt, w_fwd, w_back, conv_bias[:, None], coarse)
    return (pooled.transpose(2, 0, 1, 3), vgrad.transpose(2, 0, 1, 3),
            kgrad[:, :432].reshape(32, 27, 16), kgrad[:, 432])


def solution(mesh):
    placed = (P(None, "block", "chan", None), P(), P(), P(None, "block", "chan", None))
    return jax.shard_map(
        functools.partial(local, factors_of(mesh)),
        mesh=mesh,
        in_specs=placed,
        out_specs=(P(None, "block", "chan", None), P(None, "block", "chan", None), P(), P()),
        check_vma=False,
    )
```

```python
import functools

import jax
import jax.numpy as jnp
from jax import lax
from jax.experimental import pallas as pl
from jax.experimental.pallas import tpu as pltpu
from jax.sharding import PartitionSpec as P

MESH = pl.DeviceIdType.MESH
F32 = jnp.float32
BF16 = jnp.bfloat16
DIRECTIONS = [(i, j) for j in (-1, 1, 0) for i in (-1, 1, 0) if (i, j) != (0, 0)]


def span_out(step):
    return slice(1, 5) if step == 0 else (slice(4, 5) if step > 0 else slice(1, 2))


def span_in(step):
    return slice(1, 5) if step == 0 else (slice(0, 1) if step > 0 else slice(5, 6))


def nt_dot(a, b):
    return lax.dot_general(a, b, (((1,), (1,)), ((), ())), preferred_element_type=F32)


def far_first(n):
    return sorted(range(1, n), key=lambda k: -min(k, n - k))


def kernel(factors, volume_h, weights_h, bias_h, coarse_h, pooled_o, vgrad_o, kgrad_o, bgrad_o,
           volume_v, weights_v, bias_v, coarse_v, vol_f, coarse_f, pool_f,
           wide, shifted, cols, pre, grad, cols_back, w_back, terms, from_one, from_two, from_three, result,
           in_sem, halo_send, halo_recv, grad_send, grad_recv, stage_send, stage_recv):
    ny, nzl, nx, nzh, ncore = factors
    nblock, nchan = ny * nzl, nx * nzh * ncore
    blk, chn = lax.axis_index("block"), lax.axis_index("chan")
    y, zl = lax.div(blk, nzl), lax.rem(blk, nzl)
    x, zh, core = lax.div(chn, nzh * ncore), lax.rem(lax.div(chn, ncore), nzh), lax.rem(chn, ncore)
    n_one, n_two, n_three = nx * ncore, ny, nzh * nzl
    me_one, me_two, me_three = x * ncore + core, y, zh * nzl + zl

    def dev_one(k):
        return (blk, lax.div(k, ncore) * (nzh * ncore) + zh * ncore + lax.rem(k, ncore))

    def dev_two(k):
        return (k * nzl + zl, chn)

    def dev_three(k):
        return (y * nzl + lax.rem(k, nzl), x * (nzh * ncore) + lax.div(k, nzl) * ncore + core)

    def inside(di, dj):
        return (blk + di >= 0) & (blk + di < nblock) & (chn + dj >= 0) & (chn + dj < nchan)

    groups = ((n_one, me_one, dev_one), (n_two, me_two, dev_two), (n_three, me_three, dev_three))

    barrier = pltpu.get_barrier_semaphore()
    count = jnp.int32(n_one + n_two + n_three - 3)
    for di, dj in DIRECTIONS:
        ok = inside(di, dj)
        count = count + ok.astype(jnp.int32)

        @pl.when(ok)
        def _(di=di, dj=dj):
            pl.semaphore_signal(barrier, inc=1, device_id=(blk + di, chn + dj), device_id_type=MESH)
    loads = [pltpu.make_async_copy(src, dst, in_sem.at[i]) for i, (src, dst) in enumerate(
        ((volume_h, volume_v), (weights_h, weights_v), (bias_h, bias_v), (coarse_h, coarse_v)))]
    for load in loads:
        load.start()
    for n, me, dev in groups:
        for k in far_first(n):
            pl.semaphore_signal(barrier, inc=1, device_id=dev(lax.rem(me + k, n)), device_id_type=MESH)
    loads[0].wait()
    vol_f[...] = volume_v[...].astype(F32)
    for i in range(4):
        for j in range(4):
            wide[1 + i, 1 + j] = vol_f[:, i, j, :].astype(BF16)
    pl.semaphore_wait(barrier, count)

    def halo(buf, send, recv, which):
        di, dj = DIRECTIONS[which]
        return pltpu.make_async_remote_copy(
            src_ref=buf.at[span_out(di), span_out(dj)],
            dst_ref=buf.at[span_in(di), span_in(dj)],
            send_sem=send.at[which], recv_sem=recv.at[which],
            device_id=(blk + di, chn + dj), device_id_type=MESH)

    def halo_start(buf, send, recv):
        for which, (di, dj) in enumerate(DIRECTIONS):
            @pl.when(inside(di, dj))
            def _(which=which):
                halo(buf, send, recv, which).start()

    def halo_recv_wait(buf, send, recv):
        for which, (di, dj) in enumerate(DIRECTIONS):
            @pl.when(inside(-di, -dj))
            def _(which=which):
                halo(buf, send, recv, which).wait_recv()

    def halo_send_wait(buf, send, recv):
        for which, (di, dj) in enumerate(DIRECTIONS):
            @pl.when(inside(di, dj))
            def _(which=which):
                halo(buf, send, recv, which).wait_send()

    def clear_rim(buf):
        for di, dj in DIRECTIONS:
            @pl.when(jnp.logical_not(inside(-di, -dj)))
            def _(di=di, dj=dj):
                part = (span_in(di), span_in(dj))
                buf[part] = jnp.zeros((part[0].stop - part[0].start, part[1].stop - part[1].start) + buf.shape[2:], BF16)

    halo_start(wide, halo_send, halo_recv)

    clear_rim(wide)
    clear_rim(grad)
    cols[:, :, 432:512, :] = jnp.ones((4, 4, 80, 128), BF16)
    for load in loads[1:]:
        load.wait()
    row = lax.broadcasted_iota(jnp.int32, (64, 128), 0)
    lane = lax.broadcasted_iota(jnp.int32, (64, 128), 1)
    up_map = (lax.shift_right_logical(lane, 1) == row).astype(F32).astype(BF16)
    coarse_f[...] = coarse_v[...].astype(F32)
    ups = [[jnp.dot(coarse_f[:, i, j, :].astype(BF16), up_map, preferred_element_type=F32) * 0.125
            for j in range(2)] for i in range(2)]
    row2 = lax.broadcasted_iota(jnp.int32, (128, 256), 0)
    lane2 = lax.broadcasted_iota(jnp.int32, (128, 256), 1)
    shift_map = (row2 == jnp.where(lane2 < 128, lane2 - 1, lane2 - 127)).astype(F32).astype(BF16)
    eye = (lax.broadcasted_iota(jnp.int32, (32, 32), 0) == lax.broadcasted_iota(jnp.int32, (32, 32), 1)).astype(F32)
    bias = jnp.sum(eye * bias_v[...], axis=1, keepdims=True)
    w_t = jnp.concatenate([weights_v[...].reshape(432, 32), jnp.zeros((80, 32), BF16)], axis=0)
    w_fwd = nt_dot(eye.astype(BF16), w_t).astype(BF16)
    for d in range(3):
        w_back[16 * d:16 * d + 16, :] = jnp.concatenate(
            [weights_v[26 - 3 * s - d] for s in range(9)], axis=1)

    halo_recv_wait(wide, halo_send, halo_recv)

    for i in range(6):
        moved = jnp.dot(wide[i].reshape(96, 128), shift_map, preferred_element_type=F32).astype(BF16)
        shifted[0, i] = moved[:, :128].reshape(6, 16, 128)
        shifted[1, i] = moved[:, 128:].reshape(6, 16, 128)
    for a in range(3):
        for b in range(3):
            for d in range(3):
                t = 9 * a + 3 * b + d
                source = wide if d == 1 else shifted.at[d // 2]
                cols[:, :, 16 * t:16 * t + 16, :] = source[a:a + 4, b:b + 4]
    for i in range(4):
        for j in range(4):
            act = jnp.dot(w_fwd, cols[i, j], preferred_element_type=F32) + bias
            pre[i, j] = act
            slope = 0.2 + 0.8 * jax.nn.sigmoid(act)
            grad[1 + i, 1 + j] = (ups[i // 2][j // 2] * slope).astype(BF16)
    kacc = jnp.zeros((128, 128), F32)
    for i in range(4):
        for j in range(0, 4, 2):
            pair = jnp.concatenate([grad[1 + i, 1 + j], grad[1 + i, 2 + j]], axis=1)
            for q in range(4):
                left = jnp.concatenate([cols[i, j, 128 * q:128 * q + 128, :],
                                        cols[i, j + 1, 128 * q:128 * q + 128, :]], axis=1)
                blocks = [jnp.zeros((32, 256), BF16)] * 4
                blocks[q] = pair
                kacc = kacc + nt_dot(left, jnp.concatenate(blocks, axis=0))
    terms[...] = kacc.reshape(16, 8, 128)

    per = 16 // n_one
    own = pl.ds(me_one * per, per)

    def stage_copy(stage, group, k, src, dst):
        n, me, dev = groups[group]
        return pltpu.make_async_remote_copy(
            src_ref=src, dst_ref=dst, send_sem=stage_send.at[stage], recv_sem=stage_recv.at[stage],
            device_id=dev(lax.rem(me + k, n)), device_id_type=MESH)

    def stage_all(stage, buf, n):
        ref = buf.at[pl.ds(0, n - 1)] if stage < 3 else buf.at[pl.ds(0, (n - 1) * per)]
        return pltpu.make_async_remote_copy(
            src_ref=ref, dst_ref=ref, send_sem=stage_send.at[stage], recv_sem=stage_recv.at[stage],
            device_id=(blk, chn), device_id_type=MESH)

    def total(buf, n):
        acc = buf[0]
        for k in range(1, n):
            acc = acc + buf[k]
        return acc

    for k in far_first(n_one):
        stage_copy(0, 0, k, terms.at[pl.ds(lax.rem(me_one + k, n_one) * per, per)], from_one.at[me_one]).start()
    from_one[me_one] = terms[own]
    halo_start(grad, grad_send, grad_recv)
    halo_send_wait(wide, halo_send, halo_recv)

    stage_all(0, from_one, n_one).wait_recv()
    from_two[me_two] = total(from_one, n_one)
    for k in far_first(n_two):
        stage_copy(1, 1, k, from_two.at[me_two], from_two.at[me_two]).start()

    pool_row = lax.broadcasted_iota(jnp.int32, (128, 64), 0)
    pool_lane = lax.broadcasted_iota(jnp.int32, (128, 64), 1)
    pool_map = jnp.where(lax.shift_right_logical(pool_row, 1) == pool_lane, 0.125, 0.0).astype(F32)
    for i in range(2):
        for j in range(2):
            acc = None
            for p in range(2):
                for q in range(2):
                    v = pre[2 * i + p, 2 * j + q]
                    smooth = 0.2 * v + 0.8 * (jnp.maximum(v, 0.0) + jnp.log1p(jnp.exp(-jnp.abs(v))))
                    acc = smooth if acc is None else acc + smooth
            pool_f[:, i, j, :] = jnp.dot(acc, pool_map, precision=lax.Precision.HIGHEST, preferred_element_type=F32)
    pooled_o[...] = pool_f[...].astype(BF16)
    stage_all(0, from_one, n_one).wait_send()

    stage_all(1, from_two, n_two).wait_recv()
    from_three[me_three] = total(from_two, n_two)
    for k in far_first(n_three):
        stage_copy(2, 2, k, from_three.at[me_three], from_three.at[me_three]).start()

    stage_all(1, from_two, n_two).wait_send()
    halo_recv_wait(grad, grad_send, grad_recv)
    for a in range(3):
        for b in range(3):
            t = 3 * a + b
            cols_back[:, :, 32 * t:32 * t + 32, :] = grad[a:a + 4, b:b + 4]
    zlane = lax.broadcasted_iota(jnp.int32, (16, 128), 1)
    for i in range(4):
        for j in range(4):
            part = jnp.dot(w_back[...], cols_back[i, j], preferred_element_type=F32)
            before = jnp.where(zlane == 0, 0.0, pltpu.roll(part[:16], 1, 1))
            after = jnp.where(zlane == 127, 0.0, pltpu.roll(part[32:], 127, 1))
            vol_f[:, i, j, :] = before + part[16:32] + after
    vgrad_o[...] = vol_f[...].astype(BF16)
    halo_send_wait(grad, grad_send, grad_recv)

    stage_all(2, from_three, n_three).wait_recv()
    result[own] = total(from_three, n_three)
    for k in far_first(n_one):
        stage_copy(3, 0, k, result.at[own], result.at[own]).start()
    stage_all(2, from_three, n_three).wait_send()
    stage_all(3, result, n_one).wait_recv()
    full = result[...].reshape(128, 128)
    for q in range(4):
        part = full if q == 0 else pltpu.roll(full, 128 - 32 * q, 1)
        taps = 8 if q < 3 else 3
        kgrad_o[8 * q:8 * q + taps] = part[:16 * taps, :32].reshape(taps, 16, 32)
    bgrad_o[...] = part[48:49, :32]
    stage_all(3, result, n_one).wait_send()


def leave(pooled_v, vgrad_v, kgrad_v, bgrad_v, pooled_h, vgrad_h, kgrad_h, bgrad_h, sem):
    copies = [pltpu.make_async_copy(src, dst, sem.at[i]) for i, (src, dst) in enumerate(
        ((vgrad_v, vgrad_h), (kgrad_v, kgrad_h), (pooled_v, pooled_h), (bgrad_v, bgrad_h)))]
    for c in copies:
        c.start()
    for c in copies:
        c.wait()


def factors_of(mesh):
    nblock, nchan = mesh.shape["block"], mesh.shape["chan"]
    if (nblock, nchan) == (48, 16):
        return (8, 6, 4, 2, 2)
    return (2, nblock // 2, nchan // 4, 2, 2)


def local(factors, volume, weights, conv_bias, pooled_grad):
    ny, nzl, nx, nzh, ncore = factors
    n_one, n_two, n_three = nx * ncore, ny, nzh * nzl
    per = 16 // n_one
    vmem = pl.BlockSpec(memory_space=pltpu.VMEM)
    hbm = pl.BlockSpec(memory_space=pltpu.HBM)
    dma = pltpu.SemaphoreType.DMA
    shapes = (jax.ShapeDtypeStruct((32, 2, 2, 64), BF16), jax.ShapeDtypeStruct((16, 4, 4, 128), BF16),
              jax.ShapeDtypeStruct((27, 16, 32), F32), jax.ShapeDtypeStruct((1, 32), F32))
    outs = pl.pallas_call(
        functools.partial(kernel, factors),
        out_shape=shapes,
        in_specs=[hbm] * 4,
        out_specs=(vmem,) * 4,
        scratch_shapes=[
            pltpu.VMEM((16, 4, 4, 128), BF16),
            pltpu.VMEM((27, 16, 32), BF16),
            pltpu.VMEM((1, 32), F32),
            pltpu.VMEM((32, 2, 2, 64), BF16),
            pltpu.VMEM((16, 4, 4, 128), F32),
            pltpu.VMEM((32, 2, 2, 64), F32),
            pltpu.VMEM((32, 2, 2, 64), F32),
            pltpu.VMEM((6, 6, 16, 128), BF16),
            pltpu.VMEM((2, 6, 6, 16, 128), BF16),
            pltpu.VMEM((4, 4, 512, 128), BF16),
            pltpu.VMEM((4, 4, 32, 128), F32),
            pltpu.VMEM((6, 6, 32, 128), BF16),
            pltpu.VMEM((4, 4, 288, 128), BF16),
            pltpu.VMEM((48, 288), BF16),
            pltpu.VMEM((16, 8, 128), F32),
            pltpu.VMEM((n_one, per, 8, 128), F32),
            pltpu.VMEM((n_two, per, 8, 128), F32),
            pltpu.VMEM((n_three, per, 8, 128), F32),
            pltpu.VMEM((16, 8, 128), F32),
            dma((4,)), dma((8,)), dma((8,)), dma((8,)), dma((8,)), dma((4,)), dma((4,)),
        ],
        compiler_params=pltpu.CompilerParams(
            collective_id=0, has_side_effects=True, vmem_limit_bytes=32 * 1024 * 1024),
        name="conv_step",
    )(*[pltpu.with_memory_space_constraint(v, pltpu.HBM)
        for v in (volume, weights.transpose(1, 2, 0), conv_bias.reshape(1, 32), pooled_grad)])
    pooled, vgrad, kgrad, bgrad = pl.pallas_call(
        leave,
        out_shape=shapes,
        in_specs=[vmem] * 4,
        out_specs=(pl.BlockSpec(memory_space=pltpu.HBM),) * 4,
        scratch_shapes=[dma((4,))],
        compiler_params=pltpu.CompilerParams(vmem_limit_bytes=1024 * 1024),
        name="leave",
    )(*outs)
    return (pooled, vgrad, kgrad.transpose(2, 0, 1), bgrad.reshape(32))


def solution(mesh):
    placed = (P(None, "block", "chan", None), P(), P(), P(None, "block", "chan", None))
    return jax.shard_map(
        functools.partial(local, factors_of(mesh)),
        mesh=mesh,
        in_specs=placed,
        out_specs=(P(None, "block", "chan", None), P(None, "block", "chan", None), P(), P()),
        check_vma=False,
    )
```

```python
import functools

import jax
import jax.numpy as jnp
from jax import lax
from jax.experimental import pallas as pl
from jax.experimental.pallas import tpu as pltpu
from jax.sharding import PartitionSpec as P

MESH = pl.DeviceIdType.MESH
F32 = jnp.float32
BF16 = jnp.bfloat16
DIRECTIONS = [(0, 1), (0, -1), (1, 0), (-1, 0), (1, 1), (1, -1), (-1, 1), (-1, -1)]


def span_out(step):
    return slice(1, 5) if step == 0 else (slice(4, 5) if step > 0 else slice(1, 2))


def span_in(step):
    return slice(1, 5) if step == 0 else (slice(0, 1) if step > 0 else slice(5, 6))


def nt_dot(a, b):
    return lax.dot_general(a, b, (((1,), (1,)), ((), ())), preferred_element_type=F32)


def far_first(n):
    return sorted(range(1, n), key=lambda k: -min(k, n - k))


def kernel(factors, volume_h, weights_h, bias_h, coarse_h, pooled_o, vgrad_o, kgrad_o, bgrad_o,
           volume_v, weights_v, bias_v, coarse_v, vol_f, coarse_f, pool_f,
           wide, shifted, cols, pre, grad, cols_back, w_back, terms, from_one, from_two, from_three, result,
           in_sem, halo_send, halo_recv, grad_send, grad_recv, stage_send, stage_recv):
    ny, nzl, nx, nzh, ncore = factors
    nblock, nchan = ny * nzl, nx * nzh * ncore
    blk, chn = lax.axis_index("block"), lax.axis_index("chan")
    y, zl = lax.div(blk, nzl), lax.rem(blk, nzl)
    x, zh, core = lax.div(chn, nzh * ncore), lax.rem(lax.div(chn, ncore), nzh), lax.rem(chn, ncore)
    n_one, n_two, n_three = nx * ncore, ny, nzh * nzl
    me_one, me_two, me_three = x * ncore + core, y, zh * nzl + zl

    def dev_one(k):
        return (blk, lax.div(k, ncore) * (nzh * ncore) + zh * ncore + lax.rem(k, ncore))

    def dev_two(k):
        return (k * nzl + zl, chn)

    def dev_three(k):
        return (y * nzl + lax.rem(k, nzl), x * (nzh * ncore) + lax.div(k, nzl) * ncore + core)

    def inside(di, dj):
        return (blk + di >= 0) & (blk + di < nblock) & (chn + dj >= 0) & (chn + dj < nchan)

    groups = ((n_one, me_one, dev_one), (n_two, me_two, dev_two))
    half = (n_three - 2) // 2
    is_root = me_three < 2
    first_served = jnp.where(me_three == 0, 2 + half, 2)

    barrier = pltpu.get_barrier_semaphore()
    count = n_one + n_two - 2 + jnp.where(is_root, 1, 2)
    for di, dj in DIRECTIONS:
        ok = inside(di, dj)
        count = count + ok.astype(jnp.int32)

        @pl.when(ok)
        def _(di=di, dj=dj):
            pl.semaphore_signal(barrier, inc=1, device_id=(blk + di, chn + dj), device_id_type=MESH)
    loads = [pltpu.make_async_copy(src, dst, in_sem.at[i]) for i, (src, dst) in enumerate(
        ((volume_h, volume_v), (weights_h, weights_v), (bias_h, bias_v), (coarse_h, coarse_v)))]
    for load in loads:
        load.start()
    def greet(device):
        pl.semaphore_signal(barrier, inc=1, device_id=device, device_id_type=MESH)

    for k in far_first(n_one):
        greet(dev_one(lax.rem(me_one + k, n_one)))

    for k in far_first(n_two):
        greet(dev_two(lax.rem(me_two + k, n_two)))

    @pl.when(is_root)
    def _():
        for k in far_first(n_three):
            greet(dev_three(lax.rem(me_three + k, n_three)))

    loads[0].wait()
    vol_f[...] = volume_v[...].astype(F32)
    for i in range(4):
        for j in range(4):
            wide[1 + i, 1 + j] = vol_f[:, i, j, :].astype(BF16)
    pl.semaphore_wait(barrier, count)

    def halo(buf, send, recv, which):
        di, dj = DIRECTIONS[which]
        return pltpu.make_async_remote_copy(
            src_ref=buf.at[span_out(di), span_out(dj)],
            dst_ref=buf.at[span_in(di), span_in(dj)],
            send_sem=send.at[which], recv_sem=recv.at[which],
            device_id=(blk + di, chn + dj), device_id_type=MESH)

    def halo_start(buf, send, recv):
        for which, (di, dj) in enumerate(DIRECTIONS):
            @pl.when(inside(di, dj))
            def _(which=which):
                halo(buf, send, recv, which).start()

    def halo_recv_wait(buf, send, recv):
        for which, (di, dj) in enumerate(DIRECTIONS):
            @pl.when(inside(-di, -dj))
            def _(which=which):
                halo(buf, send, recv, which).wait_recv()

    def halo_send_wait(buf, send, recv):
        for which, (di, dj) in enumerate(DIRECTIONS):
            @pl.when(inside(di, dj))
            def _(which=which):
                halo(buf, send, recv, which).wait_send()

    def clear_rim(buf):
        for di, dj in DIRECTIONS:
            @pl.when(jnp.logical_not(inside(-di, -dj)))
            def _(di=di, dj=dj):
                part = (span_in(di), span_in(dj))
                buf[part] = jnp.zeros((part[0].stop - part[0].start, part[1].stop - part[1].start) + buf.shape[2:], BF16)

    halo_start(wide, halo_send, halo_recv)

    clear_rim(wide)
    clear_rim(grad)
    cols[:, :, 432:512, :] = jnp.ones((4, 4, 80, 128), BF16)
    for load in loads[1:]:
        load.wait()
    row = lax.broadcasted_iota(jnp.int32, (64, 128), 0)
    lane = lax.broadcasted_iota(jnp.int32, (64, 128), 1)
    up_map = (lax.shift_right_logical(lane, 1) == row).astype(F32).astype(BF16)
    coarse_f[...] = coarse_v[...].astype(F32)
    ups = [[jnp.dot(coarse_f[:, i, j, :].astype(BF16), up_map, preferred_element_type=F32) * 0.125
            for j in range(2)] for i in range(2)]
    row2 = lax.broadcasted_iota(jnp.int32, (128, 256), 0)
    lane2 = lax.broadcasted_iota(jnp.int32, (128, 256), 1)
    shift_map = (row2 == jnp.where(lane2 < 128, lane2 - 1, lane2 - 127)).astype(F32).astype(BF16)
    eye = (lax.broadcasted_iota(jnp.int32, (32, 32), 0) == lax.broadcasted_iota(jnp.int32, (32, 32), 1)).astype(F32)
    bias = jnp.sum(eye * bias_v[...], axis=1, keepdims=True)
    w_t = jnp.concatenate([weights_v[...].reshape(432, 32), jnp.zeros((80, 32), BF16)], axis=0)
    w_fwd = nt_dot(eye.astype(BF16), w_t).astype(BF16)
    for d in range(3):
        w_back[16 * d:16 * d + 16, :] = jnp.concatenate(
            [weights_v[26 - 3 * s - d] for s in range(9)], axis=1)

    sources = (shifted.at[0], wide, shifted.at[1])

    def shift(r0, r1, c0, c1):
        shape = (r1 - r0, c1 - c0, 16, 128)
        moved = jnp.dot(wide[r0:r1, c0:c1].reshape(-1, 128), shift_map, preferred_element_type=F32).astype(BF16)
        shifted[0, r0:r1, c0:c1] = moved[:, :128].reshape(shape)
        shifted[1, r0:r1, c0:c1] = moved[:, 128:].reshape(shape)

    def gather(a, b, i0, i1, j0, j1):
        for d in range(3):
            t = 9 * a + 3 * b + d
            cols[i0:i1, j0:j1, 16 * t:16 * t + 16, :] = sources[d][a + i0:a + i1, b + j0:b + j1]

    own_part = ((1, 4), (0, 4), (0, 3))
    rim_part = ((0, 1), None, (3, 4))
    shift(1, 5, 1, 5)
    for a in range(3):
        for b in range(3):
            gather(a, b, *own_part[a], *own_part[b])

    halo_recv_wait(wide, halo_send, halo_recv)

    shift(0, 1, 0, 6)
    shift(5, 6, 0, 6)
    shift(1, 5, 0, 1)
    shift(1, 5, 5, 6)
    for a in range(3):
        for b in range(3):
            if a != 1:
                gather(a, b, *rim_part[a], 0, 4)
            if b != 1:
                gather(a, b, *own_part[a], *rim_part[b])
    for i in range(4):
        for j in range(4):
            act = jnp.dot(w_fwd, cols[i, j], preferred_element_type=F32) + bias
            pre[i, j] = act
            slope = 0.2 + 0.8 * jax.nn.sigmoid(act)
            grad[1 + i, 1 + j] = (ups[i // 2][j // 2] * slope).astype(BF16)
    kacc = jnp.zeros((128, 128), F32)
    for i in range(4):
        for j in range(0, 4, 2):
            pair = jnp.concatenate([grad[1 + i, 1 + j], grad[1 + i, 2 + j]], axis=1)
            for q in range(4):
                left = jnp.concatenate([cols[i, j, 128 * q:128 * q + 128, :],
                                        cols[i, j + 1, 128 * q:128 * q + 128, :]], axis=1)
                blocks = [jnp.zeros((32, 256), BF16)] * 4
                blocks[q] = pair
                kacc = kacc + nt_dot(left, jnp.concatenate(blocks, axis=0))
    terms[...] = kacc.reshape(16, 8, 128)

    per = 16 // n_one
    own = pl.ds(me_one * per, per)

    def copy_to(stage, device, src, dst):
        return pltpu.make_async_remote_copy(
            src_ref=src, dst_ref=dst, send_sem=stage_send.at[stage], recv_sem=stage_recv.at[stage],
            device_id=device, device_id_type=MESH)

    def shards(stage, number):
        ref = terms.at[pl.ds(0, number * per)] if number * per <= 16 else from_three.at[pl.ds(0, number)]
        return copy_to(stage, (blk, chn), ref, ref)

    def total(buf, n):
        acc = buf[0]
        for k in range(1, n):
            acc = acc + buf[k]
        return acc

    for k in far_first(n_one):
        other = lax.rem(me_one + k, n_one)
        copy_to(0, dev_one(other), terms.at[pl.ds(other * per, per)], from_one.at[me_one]).start()
    from_one[me_one] = terms[own]
    halo_start(grad, grad_send, grad_recv)
    halo_send_wait(wide, halo_send, halo_recv)

    shards(0, n_one - 1).wait_recv()
    from_two[me_two] = total(from_one, n_one)
    for k in far_first(n_two):
        copy_to(2, dev_two(lax.rem(me_two + k, n_two)), from_two.at[me_two], from_two.at[me_two]).start()

    pool_row = lax.broadcasted_iota(jnp.int32, (128, 64), 0)
    pool_lane = lax.broadcasted_iota(jnp.int32, (128, 64), 1)
    pool_map = jnp.where(lax.shift_right_logical(pool_row, 1) == pool_lane, 0.125, 0.0).astype(F32)
    def smooth_row(i, carry):
        v = pre[i]
        pre[i] = 0.2 * v + 0.8 * (jnp.maximum(v, 0.0) + jnp.log1p(jnp.exp(-jnp.abs(v))))
        return carry

    lax.fori_loop(0, 4, smooth_row, 0)
    sums = jnp.concatenate([pre[2 * i, 2 * j] + pre[2 * i, 2 * j + 1] + pre[2 * i + 1, 2 * j] + pre[2 * i + 1, 2 * j + 1]
                            for i in range(2) for j in range(2)], axis=0)
    means = jnp.dot(sums, pool_map, precision=lax.Precision.HIGHEST, preferred_element_type=F32)
    for i in range(2):
        for j in range(2):
            pool_f[:, i, j, :] = means[64 * i + 32 * j:64 * i + 32 * j + 32]
    pooled_o[...] = pool_f[...].astype(BF16)
    shards(0, n_one - 1).wait_send()

    shards(2, n_two - 1).wait_recv()
    from_three[me_three] = total(from_two, n_two)
    for root in range(2):
        @pl.when(me_three != root)
        def _(root=root):
            copy_to(1, dev_three(root), from_three.at[me_three], from_three.at[me_three]).start()
    shards(2, n_two - 1).wait_send()

    halo_recv_wait(grad, grad_send, grad_recv)
    for a in range(3):
        for b in range(3):
            t = 3 * a + b
            cols_back[:, :, 32 * t:32 * t + 32, :] = grad[a:a + 4, b:b + 4]
    zlane = lax.broadcasted_iota(jnp.int32, (16, 128), 1)
    def back_row(i, carry):
        for j in range(4):
            part = jnp.dot(w_back[...], cols_back[i, j], preferred_element_type=F32)
            before = jnp.where(zlane == 0, 0.0, pltpu.roll(part[:16], 1, 1))
            after = jnp.where(zlane == 127, 0.0, pltpu.roll(part[32:], 127, 1))
            vol_f[:, i, j, :] = before + part[16:32] + after
        return carry

    lax.fori_loop(0, 4, back_row, 0)
    vgrad_o[...] = vol_f[...].astype(BF16)
    halo_send_wait(grad, grad_send, grad_recv)

    @pl.when(is_root)
    def _():
        shards(1, 1).wait_send()
        shards(1, n_three - 1).wait_recv()
        result[own] = total(from_three, n_three)

    @pl.when(jnp.logical_not(is_root))
    def _():
        shards(1, 2).wait_send()
        shards(4, 1).wait_recv()

    for k in far_first(n_one):
        copy_to(3, dev_one(lax.rem(me_one + k, n_one)), result.at[own], result.at[own]).start()

    @pl.when(is_root)
    def _():
        for k in range(half):
            copy_to(4, dev_three(first_served + k), result.at[own], result.at[own]).start()

    shards(3, n_one - 1).wait_recv()
    full = result[...].reshape(128, 128)
    for q in range(4):
        part = full if q == 0 else pltpu.roll(full, 128 - 32 * q, 1)
        taps = 8 if q < 3 else 3
        kgrad_o[8 * q:8 * q + taps] = part[:16 * taps, :32].reshape(taps, 16, 32)
    bgrad_o[...] = part[48:49, :32]
    shards(3, n_one - 1).wait_send()

    @pl.when(is_root)
    def _():
        shards(4, half).wait_send()


def leave(pooled_v, vgrad_v, kgrad_v, bgrad_v, pooled_h, vgrad_h, kgrad_h, bgrad_h, sem):
    copies = [pltpu.make_async_copy(src, dst, sem.at[i]) for i, (src, dst) in enumerate(
        ((vgrad_v, vgrad_h), (kgrad_v, kgrad_h), (pooled_v, pooled_h), (bgrad_v, bgrad_h)))]
    for c in copies:
        c.start()
    for c in copies:
        c.wait()


def factors_of(mesh):
    nblock, nchan = mesh.shape["block"], mesh.shape["chan"]
    if (nblock, nchan) == (48, 16):
        return (8, 6, 4, 2, 2)
    return (2, nblock // 2, nchan // 4, 2, 2)


def local(factors, volume, weights, conv_bias, pooled_grad):
    ny, nzl, nx, nzh, ncore = factors
    n_one, n_two, n_three = nx * ncore, ny, nzh * nzl
    per = 16 // n_one
    vmem = pl.BlockSpec(memory_space=pltpu.VMEM)
    hbm = pl.BlockSpec(memory_space=pltpu.HBM)
    dma = pltpu.SemaphoreType.DMA
    shapes = (jax.ShapeDtypeStruct((32, 2, 2, 64), BF16), jax.ShapeDtypeStruct((16, 4, 4, 128), BF16),
              jax.ShapeDtypeStruct((27, 16, 32), F32), jax.ShapeDtypeStruct((1, 32), F32))
    outs = pl.pallas_call(
        functools.partial(kernel, factors),
        out_shape=shapes,
        in_specs=[hbm] * 4,
        out_specs=(vmem,) * 4,
        scratch_shapes=[
            pltpu.VMEM((16, 4, 4, 128), BF16),
            pltpu.VMEM((27, 16, 32), BF16),
            pltpu.VMEM((1, 32), F32),
            pltpu.VMEM((32, 2, 2, 64), BF16),
            pltpu.VMEM((16, 4, 4, 128), F32),
            pltpu.VMEM((32, 2, 2, 64), F32),
            pltpu.VMEM((32, 2, 2, 64), F32),
            pltpu.VMEM((6, 6, 16, 128), BF16),
            pltpu.VMEM((2, 6, 6, 16, 128), BF16),
            pltpu.VMEM((4, 4, 512, 128), BF16),
            pltpu.VMEM((4, 4, 32, 128), F32),
            pltpu.VMEM((6, 6, 32, 128), BF16),
            pltpu.VMEM((4, 4, 288, 128), BF16),
            pltpu.VMEM((48, 288), BF16),
            pltpu.VMEM((16, 8, 128), F32),
            pltpu.VMEM((n_one, per, 8, 128), F32),
            pltpu.VMEM((n_two, per, 8, 128), F32),
            pltpu.VMEM((n_three, per, 8, 128), F32),
            pltpu.VMEM((16, 8, 128), F32),
            dma((4,)), dma((8,)), dma((8,)), dma((8,)), dma((8,)), dma((5,)), dma((5,)),
        ],
        compiler_params=pltpu.CompilerParams(
            collective_id=0, has_side_effects=True, vmem_limit_bytes=32 * 1024 * 1024),
        name="conv_step",
    )(*[pltpu.with_memory_space_constraint(v, pltpu.HBM)
        for v in (volume, weights.transpose(1, 2, 0), conv_bias.reshape(1, 32), pooled_grad)])
    pooled, vgrad, kgrad, bgrad = pl.pallas_call(
        leave,
        out_shape=shapes,
        in_specs=[vmem] * 4,
        out_specs=(pl.BlockSpec(memory_space=pltpu.HBM),) * 4,
        scratch_shapes=[dma((4,))],
        compiler_params=pltpu.CompilerParams(vmem_limit_bytes=1024 * 1024),
        name="leave",
    )(*outs)
    return (pooled, vgrad, kgrad.transpose(2, 0, 1), bgrad.reshape(32))


def solution(mesh):
    placed = (P(None, "block", "chan", None), P(), P(), P(None, "block", "chan", None))
    return jax.shard_map(
        functools.partial(local, factors_of(mesh)),
        mesh=mesh,
        in_specs=placed,
        out_specs=(P(None, "block", "chan", None), P(None, "block", "chan", None), P(), P()),
        check_vma=False,
    )
```

```python
import functools

import jax
import jax.numpy as jnp
from jax import lax
from jax.experimental import pallas as pl
from jax.experimental.pallas import tpu as pltpu
from jax.sharding import PartitionSpec as P

MESH = pl.DeviceIdType.MESH
F32 = jnp.float32
BF16 = jnp.bfloat16
DIRECTIONS = [(0, 1), (0, -1), (1, 0), (-1, 0), (1, 1), (1, -1), (-1, 1), (-1, -1)]


def span_out(step):
    return slice(1, 5) if step == 0 else (slice(4, 5) if step > 0 else slice(1, 2))


def span_in(step):
    return slice(1, 5) if step == 0 else (slice(0, 1) if step > 0 else slice(5, 6))


def nt_dot(a, b):
    return lax.dot_general(a, b, (((1,), (1,)), ((), ())), preferred_element_type=F32)


def far_first(n):
    return sorted(range(1, n), key=lambda k: -min(k, n - k))


def kernel(factors, volume_h, weights_h, bias_h, coarse_h, pooled_o, vgrad_o, kgrad_o, bgrad_o,
           volume_v, weights_v, bias_v, coarse_v, vol_f, coarse_f, pool_f,
           wide, shifted, cols, pre, grad, cols_back, w_back, terms, from_one, from_two, from_three, result,
           in_sem, halo_send, halo_recv, grad_send, grad_recv, stage_send, stage_recv):
    ny, nzl, nx, nzh, ncore = factors
    nblock, nchan = ny * nzl, nx * nzh * ncore
    blk, chn = lax.axis_index("block"), lax.axis_index("chan")
    y, zl = lax.div(blk, nzl), lax.rem(blk, nzl)
    x, zh, core = lax.div(chn, nzh * ncore), lax.rem(lax.div(chn, ncore), nzh), lax.rem(chn, ncore)
    n_one, n_two, n_three = nx * ncore, ny, nzh * nzl
    me_one, me_two, me_three = x * ncore + core, y, zh * nzl + zl

    def dev_one(k):
        return (blk, lax.div(k, ncore) * (nzh * ncore) + zh * ncore + lax.rem(k, ncore))

    def dev_two(k):
        return (k * nzl + zl, chn)

    def dev_three(k):
        return (y * nzl + lax.rem(k, nzl), x * (nzh * ncore) + lax.div(k, nzl) * ncore + core)

    def inside(di, dj):
        return (blk + di >= 0) & (blk + di < nblock) & (chn + dj >= 0) & (chn + dj < nchan)

    groups = ((n_one, me_one, dev_one), (n_two, me_two, dev_two))
    half = (n_three - 2) // 2
    is_root = me_three < 2
    first_served = jnp.where(me_three == 0, 2 + half, 2)

    barrier = pltpu.get_barrier_semaphore()
    count = n_one + n_two - 2 + jnp.where(is_root, 1, 2)
    for di, dj in DIRECTIONS:
        ok = inside(di, dj)
        count = count + ok.astype(jnp.int32)

        @pl.when(ok)
        def _(di=di, dj=dj):
            pl.semaphore_signal(barrier, inc=1, device_id=(blk + di, chn + dj), device_id_type=MESH)
    def greet(device):
        pl.semaphore_signal(barrier, inc=1, device_id=device, device_id_type=MESH)

    for k in far_first(n_one):
        greet(dev_one(lax.rem(me_one + k, n_one)))

    loads = [pltpu.make_async_copy(src, dst, in_sem.at[i]) for i, (src, dst) in enumerate(
        ((volume_h, volume_v), (weights_h, weights_v), (bias_h, bias_v), (coarse_h, coarse_v)))]
    for load in loads:
        load.start()
    for k in far_first(n_two):
        greet(dev_two(lax.rem(me_two + k, n_two)))

    @pl.when(is_root)
    def _():
        for k in far_first(n_three):
            greet(dev_three(lax.rem(me_three + k, n_three)))

    loads[0].wait()
    vol_f[...] = volume_v[...].astype(F32)
    for i in range(4):
        for j in range(4):
            wide[1 + i, 1 + j] = vol_f[:, i, j, :].astype(BF16)
    pl.semaphore_wait(barrier, count)

    def halo(buf, send, recv, which):
        di, dj = DIRECTIONS[which]
        return pltpu.make_async_remote_copy(
            src_ref=buf.at[span_out(di), span_out(dj)],
            dst_ref=buf.at[span_in(di), span_in(dj)],
            send_sem=send.at[which], recv_sem=recv.at[which],
            device_id=(blk + di, chn + dj), device_id_type=MESH)

    def halo_start(buf, send, recv):
        for which, (di, dj) in enumerate(DIRECTIONS):
            @pl.when(inside(di, dj))
            def _(which=which):
                halo(buf, send, recv, which).start()

    def halo_recv_wait(buf, send, recv):
        for which, (di, dj) in enumerate(DIRECTIONS):
            @pl.when(inside(-di, -dj))
            def _(which=which):
                halo(buf, send, recv, which).wait_recv()

    def halo_send_wait(buf, send, recv):
        for which, (di, dj) in enumerate(DIRECTIONS):
            @pl.when(inside(di, dj))
            def _(which=which):
                halo(buf, send, recv, which).wait_send()

    def clear_rim(buf):
        for di, dj in DIRECTIONS:
            @pl.when(jnp.logical_not(inside(-di, -dj)))
            def _(di=di, dj=dj):
                part = (span_in(di), span_in(dj))
                buf[part] = jnp.zeros((part[0].stop - part[0].start, part[1].stop - part[1].start) + buf.shape[2:], BF16)

    halo_start(wide, halo_send, halo_recv)

    clear_rim(wide)
    clear_rim(grad)
    cols[:, :, 432:512, :] = jnp.ones((4, 4, 80, 128), BF16)
    for load in loads[1:]:
        load.wait()
    row = lax.broadcasted_iota(jnp.int32, (64, 128), 0)
    lane = lax.broadcasted_iota(jnp.int32, (64, 128), 1)
    up_map = (lax.shift_right_logical(lane, 1) == row).astype(F32).astype(BF16)
    coarse_f[...] = coarse_v[...].astype(F32)
    ups = [[jnp.dot(coarse_f[:, i, j, :].astype(BF16), up_map, preferred_element_type=F32) * 0.125
            for j in range(2)] for i in range(2)]
    row2 = lax.broadcasted_iota(jnp.int32, (128, 256), 0)
    lane2 = lax.broadcasted_iota(jnp.int32, (128, 256), 1)
    shift_map = (row2 == jnp.where(lane2 < 128, lane2 - 1, lane2 - 127)).astype(F32).astype(BF16)
    eye = (lax.broadcasted_iota(jnp.int32, (32, 32), 0) == lax.broadcasted_iota(jnp.int32, (32, 32), 1)).astype(F32)
    bias = jnp.sum(eye * bias_v[...], axis=1, keepdims=True)
    w_t = jnp.concatenate([weights_v[...].reshape(432, 32), jnp.zeros((80, 32), BF16)], axis=0)
    w_fwd = nt_dot(eye.astype(BF16), w_t).astype(BF16)
    for d in range(3):
        w_back[16 * d:16 * d + 16, :] = jnp.concatenate(
            [weights_v[26 - 3 * s - d] for s in range(9)], axis=1)

    sources = (shifted.at[0], wide, shifted.at[1])

    def shift(r0, r1, c0, c1):
        shape = (r1 - r0, c1 - c0, 16, 128)
        moved = jnp.dot(wide[r0:r1, c0:c1].reshape(-1, 128), shift_map, preferred_element_type=F32).astype(BF16)
        shifted[0, r0:r1, c0:c1] = moved[:, :128].reshape(shape)
        shifted[1, r0:r1, c0:c1] = moved[:, 128:].reshape(shape)

    def gather(a, b, i0, i1, j0, j1):
        for d in range(3):
            t = 9 * a + 3 * b + d
            cols[i0:i1, j0:j1, 16 * t:16 * t + 16, :] = sources[d][a + i0:a + i1, b + j0:b + j1]

    own_part = ((1, 4), (0, 4), (0, 3))
    rim_part = ((0, 1), None, (3, 4))
    shift(1, 5, 1, 5)
    for a in range(3):
        for b in range(3):
            gather(a, b, *own_part[a], *own_part[b])

    halo_recv_wait(wide, halo_send, halo_recv)

    shift(0, 1, 0, 6)
    shift(5, 6, 0, 6)
    shift(1, 5, 0, 1)
    shift(1, 5, 5, 6)
    for a in range(3):
        for b in range(3):
            if a != 1:
                gather(a, b, *rim_part[a], 0, 4)
            if b != 1:
                gather(a, b, *own_part[a], *rim_part[b])
    for i in range(4):
        for j in range(4):
            act = jnp.dot(w_fwd, cols[i, j], preferred_element_type=F32) + bias
            pre[i, j] = act
            slope = 0.2 + 0.8 * jax.nn.sigmoid(act)
            grad[1 + i, 1 + j] = (ups[i // 2][j // 2] * slope).astype(BF16)
    kacc = jnp.zeros((128, 128), F32)
    for i in range(4):
        for j in range(0, 4, 2):
            pair = jnp.concatenate([grad[1 + i, 1 + j], grad[1 + i, 2 + j]], axis=1)
            for q in range(4):
                left = jnp.concatenate([cols[i, j, 128 * q:128 * q + 128, :],
                                        cols[i, j + 1, 128 * q:128 * q + 128, :]], axis=1)
                blocks = [jnp.zeros((32, 256), BF16)] * 4
                blocks[q] = pair
                kacc = kacc + nt_dot(left, jnp.concatenate(blocks, axis=0))
    terms[...] = kacc.reshape(16, 8, 128)

    per = 16 // n_one
    own = pl.ds(me_one * per, per)

    def copy_to(stage, device, src, dst):
        return pltpu.make_async_remote_copy(
            src_ref=src, dst_ref=dst, send_sem=stage_send.at[stage], recv_sem=stage_recv.at[stage],
            device_id=device, device_id_type=MESH)

    def shards(stage, number):
        ref = terms.at[pl.ds(0, number * per)] if number * per <= 16 else from_three.at[pl.ds(0, number)]
        return copy_to(stage, (blk, chn), ref, ref)

    def total(buf, n):
        acc = buf[0]
        for k in range(1, n):
            acc = acc + buf[k]
        return acc

    for k in far_first(n_one):
        other = lax.rem(me_one + k, n_one)
        copy_to(0, dev_one(other), terms.at[pl.ds(other * per, per)], from_one.at[me_one]).start()
    from_one[me_one] = terms[own]
    halo_start(grad, grad_send, grad_recv)
    halo_send_wait(wide, halo_send, halo_recv)

    shards(0, n_one - 1).wait_recv()
    from_two[me_two] = total(from_one, n_one)
    for k in far_first(n_two):
        copy_to(2, dev_two(lax.rem(me_two + k, n_two)), from_two.at[me_two], from_two.at[me_two]).start()

    pool_row = lax.broadcasted_iota(jnp.int32, (128, 64), 0)
    pool_lane = lax.broadcasted_iota(jnp.int32, (128, 64), 1)
    pool_map = jnp.where(lax.shift_right_logical(pool_row, 1) == pool_lane, 0.125, 0.0).astype(F32)
    def smooth_row(i, carry):
        v = pre[i]
        pre[i] = 0.2 * v + 0.8 * (jnp.maximum(v, 0.0) + jnp.log1p(jnp.exp(-jnp.abs(v))))
        return carry

    lax.fori_loop(0, 4, smooth_row, 0)
    sums = jnp.concatenate([pre[2 * i, 2 * j] + pre[2 * i, 2 * j + 1] + pre[2 * i + 1, 2 * j] + pre[2 * i + 1, 2 * j + 1]
                            for i in range(2) for j in range(2)], axis=0)
    means = jnp.dot(sums, pool_map, precision=lax.Precision.HIGHEST, preferred_element_type=F32)
    for i in range(2):
        for j in range(2):
            pool_f[:, i, j, :] = means[64 * i + 32 * j:64 * i + 32 * j + 32]
    pooled_o[...] = pool_f[...].astype(BF16)
    shards(0, n_one - 1).wait_send()

    shards(2, n_two - 1).wait_recv()
    from_three[me_three] = total(from_two, n_two)
    for root in range(2):
        @pl.when(me_three != root)
        def _(root=root):
            copy_to(1, dev_three(root), from_three.at[me_three], from_three.at[me_three]).start()
    shards(2, n_two - 1).wait_send()

    halo_recv_wait(grad, grad_send, grad_recv)
    for a in range(3):
        for b in range(3):
            t = 3 * a + b
            cols_back[:, :, 32 * t:32 * t + 32, :] = grad[a:a + 4, b:b + 4]
    zlane = lax.broadcasted_iota(jnp.int32, (16, 128), 1)
    def back_row(i, carry):
        for j in range(4):
            part = jnp.dot(w_back[...], cols_back[i, j], preferred_element_type=F32)
            before = jnp.where(zlane == 0, 0.0, pltpu.roll(part[:16], 1, 1))
            after = jnp.where(zlane == 127, 0.0, pltpu.roll(part[32:], 127, 1))
            vol_f[:, i, j, :] = before + part[16:32] + after
        return carry

    lax.fori_loop(0, 4, back_row, 0)
    vgrad_o[...] = vol_f[...].astype(BF16)
    halo_send_wait(grad, grad_send, grad_recv)

    @pl.when(is_root)
    def _():
        shards(1, 1).wait_send()
        shards(1, n_three - 1).wait_recv()
        result[own] = total(from_three, n_three)

    @pl.when(jnp.logical_not(is_root))
    def _():
        shards(1, 2).wait_send()
        shards(4, 1).wait_recv()

    for k in far_first(n_one):
        copy_to(3, dev_one(lax.rem(me_one + k, n_one)), result.at[own], result.at[own]).start()

    @pl.when(is_root)
    def _():
        for k in range(half):
            copy_to(4, dev_three(first_served + k), result.at[own], result.at[own]).start()

    shards(3, n_one - 1).wait_recv()
    full = result[...].reshape(128, 128)
    for q in range(4):
        part = full if q == 0 else pltpu.roll(full, 128 - 32 * q, 1)
        taps = 8 if q < 3 else 3
        kgrad_o[8 * q:8 * q + taps] = part[:16 * taps, :32].reshape(taps, 16, 32)
    bgrad_o[...] = part[48:49, :32]
    shards(3, n_one - 1).wait_send()

    @pl.when(is_root)
    def _():
        shards(4, half).wait_send()


def leave(pooled_v, vgrad_v, kgrad_v, bgrad_v, pooled_h, vgrad_h, kgrad_h, bgrad_h, sem):
    copies = [pltpu.make_async_copy(src, dst, sem.at[i]) for i, (src, dst) in enumerate(
        ((vgrad_v, vgrad_h), (kgrad_v, kgrad_h), (pooled_v, pooled_h), (bgrad_v, bgrad_h)))]
    for c in copies:
        c.start()
    for c in copies:
        c.wait()


def factors_of(mesh):
    nblock, nchan = mesh.shape["block"], mesh.shape["chan"]
    if (nblock, nchan) == (48, 16):
        return (8, 6, 4, 2, 2)
    return (2, nblock // 2, nchan // 4, 2, 2)


def local(factors, volume, weights, conv_bias, pooled_grad):
    ny, nzl, nx, nzh, ncore = factors
    n_one, n_two, n_three = nx * ncore, ny, nzh * nzl
    per = 16 // n_one
    vmem = pl.BlockSpec(memory_space=pltpu.VMEM)
    hbm = pl.BlockSpec(memory_space=pltpu.HBM)
    dma = pltpu.SemaphoreType.DMA
    shapes = (jax.ShapeDtypeStruct((32, 2, 2, 64), BF16), jax.ShapeDtypeStruct((16, 4, 4, 128), BF16),
              jax.ShapeDtypeStruct((27, 16, 32), F32), jax.ShapeDtypeStruct((1, 32), F32))
    outs = pl.pallas_call(
        functools.partial(kernel, factors),
        out_shape=shapes,
        in_specs=[hbm] * 4,
        out_specs=(vmem,) * 4,
        scratch_shapes=[
            pltpu.VMEM((16, 4, 4, 128), BF16),
            pltpu.VMEM((27, 16, 32), BF16),
            pltpu.VMEM((1, 32), F32),
            pltpu.VMEM((32, 2, 2, 64), BF16),
            pltpu.VMEM((16, 4, 4, 128), F32),
            pltpu.VMEM((32, 2, 2, 64), F32),
            pltpu.VMEM((32, 2, 2, 64), F32),
            pltpu.VMEM((6, 6, 16, 128), BF16),
            pltpu.VMEM((2, 6, 6, 16, 128), BF16),
            pltpu.VMEM((4, 4, 512, 128), BF16),
            pltpu.VMEM((4, 4, 32, 128), F32),
            pltpu.VMEM((6, 6, 32, 128), BF16),
            pltpu.VMEM((4, 4, 288, 128), BF16),
            pltpu.VMEM((48, 288), BF16),
            pltpu.VMEM((16, 8, 128), F32),
            pltpu.VMEM((n_one, per, 8, 128), F32),
            pltpu.VMEM((n_two, per, 8, 128), F32),
            pltpu.VMEM((n_three, per, 8, 128), F32),
            pltpu.VMEM((16, 8, 128), F32),
            dma((4,)), dma((8,)), dma((8,)), dma((8,)), dma((8,)), dma((5,)), dma((5,)),
        ],
        compiler_params=pltpu.CompilerParams(
            collective_id=0, has_side_effects=True, vmem_limit_bytes=32 * 1024 * 1024),
        name="conv_step",
    )(*[pltpu.with_memory_space_constraint(v, pltpu.HBM)
        for v in (volume, weights.transpose(1, 2, 0), conv_bias.reshape(1, 32), pooled_grad)])
    pooled, vgrad, kgrad, bgrad = pl.pallas_call(
        leave,
        out_shape=shapes,
        in_specs=[vmem] * 4,
        out_specs=(pl.BlockSpec(memory_space=pltpu.HBM),) * 4,
        scratch_shapes=[dma((4,))],
        compiler_params=pltpu.CompilerParams(vmem_limit_bytes=1024 * 1024),
        name="leave",
    )(*outs)
    return (pooled, vgrad, kgrad.transpose(2, 0, 1), bgrad.reshape(32))


def solution(mesh):
    placed = (P(None, "block", "chan", None), P(), P(), P(None, "block", "chan", None))
    return jax.shard_map(
        functools.partial(local, factors_of(mesh)),
        mesh=mesh,
        in_specs=placed,
        out_specs=(P(None, "block", "chan", None), P(None, "block", "chan", None), P(), P()),
        check_vma=False,
    )
```

```python
import functools

import jax
import jax.numpy as jnp
from jax import lax
from jax.experimental import pallas as pl
from jax.experimental.pallas import tpu as pltpu
from jax.sharding import PartitionSpec as P

MESH = pl.DeviceIdType.MESH
F32 = jnp.float32
BF16 = jnp.bfloat16
DIRECTIONS = [(0, 1), (0, -1), (1, 0), (-1, 0), (1, 1), (1, -1), (-1, 1), (-1, -1)]


def span_out(step):
    return slice(1, 5) if step == 0 else (slice(4, 5) if step > 0 else slice(1, 2))


def span_in(step):
    return slice(1, 5) if step == 0 else (slice(0, 1) if step > 0 else slice(5, 6))


def nt_dot(a, b):
    return lax.dot_general(a, b, (((1,), (1,)), ((), ())), preferred_element_type=F32)


def far_first(n):
    return sorted(range(1, n), key=lambda k: -min(k, n - k))


def kernel(factors, volume_h, weights_h, bias_h, coarse_h, pooled_o, vgrad_o, kgrad_o, bgrad_o,
           volume_v, weights_v, bias_v, coarse_v, vol_f, coarse_f, pool_f,
           wide, shifted, cols, pre, grad, cols_back, w_back, terms, from_one, from_two, from_three, result,
           in_sem, halo_send, halo_recv, grad_send, grad_recv, stage_send, stage_recv):
    ny, nzl, nx, nzh, ncore = factors
    nblock, nchan = ny * nzl, nx * nzh * ncore
    blk, chn = lax.axis_index("block"), lax.axis_index("chan")
    y, zl = lax.div(blk, nzl), lax.rem(blk, nzl)
    x, zh, core = lax.div(chn, nzh * ncore), lax.rem(lax.div(chn, ncore), nzh), lax.rem(chn, ncore)
    n_one, n_two, n_three = nx * ncore, ny, nzh * nzl
    me_one, me_two, me_three = x * ncore + core, y, zh * nzl + zl

    def dev_one(k):
        return (blk, lax.div(k, ncore) * (nzh * ncore) + zh * ncore + lax.rem(k, ncore))

    def dev_two(k):
        return (k * nzl + zl, chn)

    def dev_three(k):
        return (y * nzl + lax.rem(k, nzl), x * (nzh * ncore) + lax.div(k, nzl) * ncore + core)

    def inside(di, dj):
        return (blk + di >= 0) & (blk + di < nblock) & (chn + dj >= 0) & (chn + dj < nchan)

    groups = ((n_one, me_one, dev_one), (n_two, me_two, dev_two))
    half = (n_three - 2) // 2
    is_root = me_three < 2
    first_served = jnp.where(me_three == 0, 2 + half, 2)

    barrier = pltpu.get_barrier_semaphore()
    count = n_one + n_two - 2 + jnp.where(is_root, 1, 2)
    for di, dj in DIRECTIONS:
        ok = inside(di, dj)
        count = count + ok.astype(jnp.int32)

        @pl.when(ok)
        def _(di=di, dj=dj):
            pl.semaphore_signal(barrier, inc=1, device_id=(blk + di, chn + dj), device_id_type=MESH)
    loads = [pltpu.make_async_copy(src, dst, in_sem.at[i]) for i, (src, dst) in enumerate(
        ((volume_h, volume_v), (weights_h, weights_v), (bias_h, bias_v), (coarse_h, coarse_v)))]
    for load in loads:
        load.start()
    def greet(device):
        pl.semaphore_signal(barrier, inc=1, device_id=device, device_id_type=MESH)

    for k in far_first(n_one):
        greet(dev_one(lax.rem(me_one + k, n_one)))

    for k in far_first(n_two):
        greet(dev_two(lax.rem(me_two + k, n_two)))

    @pl.when(is_root)
    def _():
        for k in far_first(n_three):
            greet(dev_three(lax.rem(me_three + k, n_three)))

    loads[0].wait()
    vol_f[...] = volume_v[...].astype(F32)
    for i in range(4):
        for j in range(4):
            wide[1 + i, 1 + j] = vol_f[:, i, j, :].astype(BF16)
    pl.semaphore_wait(barrier, count)

    def halo(buf, send, recv, which):
        di, dj = DIRECTIONS[which]
        return pltpu.make_async_remote_copy(
            src_ref=buf.at[span_out(di), span_out(dj)],
            dst_ref=buf.at[span_in(di), span_in(dj)],
            send_sem=send.at[which], recv_sem=recv.at[which],
            device_id=(blk + di, chn + dj), device_id_type=MESH)

    def halo_start(buf, send, recv):
        for which, (di, dj) in enumerate(DIRECTIONS):
            @pl.when(inside(di, dj))
            def _(which=which):
                halo(buf, send, recv, which).start()

    def halo_recv_wait(buf, send, recv):
        for which, (di, dj) in enumerate(DIRECTIONS):
            @pl.when(inside(-di, -dj))
            def _(which=which):
                halo(buf, send, recv, which).wait_recv()

    def halo_send_wait(buf, send, recv):
        for which, (di, dj) in enumerate(DIRECTIONS):
            @pl.when(inside(di, dj))
            def _(which=which):
                halo(buf, send, recv, which).wait_send()

    def clear_rim(buf):
        for di, dj in DIRECTIONS:
            @pl.when(jnp.logical_not(inside(-di, -dj)))
            def _(di=di, dj=dj):
                part = (span_in(di), span_in(dj))
                buf[part] = jnp.zeros((part[0].stop - part[0].start, part[1].stop - part[1].start) + buf.shape[2:], BF16)

    halo_start(wide, halo_send, halo_recv)

    clear_rim(wide)
    clear_rim(grad)
    cols[:, :, 432:512, :] = jnp.ones((4, 4, 80, 128), BF16)
    for load in loads[1:]:
        load.wait()
    row = lax.broadcasted_iota(jnp.int32, (64, 128), 0)
    lane = lax.broadcasted_iota(jnp.int32, (64, 128), 1)
    up_map = (lax.shift_right_logical(lane, 1) == row).astype(F32).astype(BF16)
    coarse_f[...] = coarse_v[...].astype(F32)
    ups = [[jnp.dot(coarse_f[:, i, j, :].astype(BF16), up_map, preferred_element_type=F32) * 0.125
            for j in range(2)] for i in range(2)]
    row2 = lax.broadcasted_iota(jnp.int32, (128, 256), 0)
    lane2 = lax.broadcasted_iota(jnp.int32, (128, 256), 1)
    shift_map = (row2 == jnp.where(lane2 < 128, lane2 - 1, lane2 - 127)).astype(F32).astype(BF16)
    eye = (lax.broadcasted_iota(jnp.int32, (32, 32), 0) == lax.broadcasted_iota(jnp.int32, (32, 32), 1)).astype(F32)
    bias = jnp.sum(eye * bias_v[...], axis=1, keepdims=True)
    w_t = jnp.concatenate([weights_v[...].reshape(432, 32), jnp.zeros((80, 32), BF16)], axis=0)
    w_fwd = nt_dot(eye.astype(BF16), w_t).astype(BF16)
    for d in range(3):
        w_back[16 * d:16 * d + 16, :] = jnp.concatenate(
            [weights_v[26 - 3 * s - d] for s in range(9)], axis=1)

    sources = (shifted.at[0], wide, shifted.at[1])

    def shift(r0, r1, c0, c1):
        shape = (r1 - r0, c1 - c0, 16, 128)
        moved = jnp.dot(wide[r0:r1, c0:c1].reshape(-1, 128), shift_map, preferred_element_type=F32).astype(BF16)
        shifted[0, r0:r1, c0:c1] = moved[:, :128].reshape(shape)
        shifted[1, r0:r1, c0:c1] = moved[:, 128:].reshape(shape)

    def gather(a, b, i0, i1, j0, j1):
        for d in range(3):
            t = 9 * a + 3 * b + d
            cols[i0:i1, j0:j1, 16 * t:16 * t + 16, :] = sources[d][a + i0:a + i1, b + j0:b + j1]

    own_part = ((1, 4), (0, 4), (0, 3))
    rim_part = ((0, 1), None, (3, 4))
    shift(1, 5, 1, 5)
    for a in range(3):
        for b in range(3):
            gather(a, b, *own_part[a], *own_part[b])

    halo_recv_wait(wide, halo_send, halo_recv)

    shift(0, 1, 0, 6)
    shift(5, 6, 0, 6)
    shift(1, 5, 0, 1)
    shift(1, 5, 5, 6)
    for a in range(3):
        for b in range(3):
            if a != 1:
                gather(a, b, *rim_part[a], 0, 4)
            if b != 1:
                gather(a, b, *own_part[a], *rim_part[b])
    for i in range(4):
        for j in range(4):
            act = jnp.dot(w_fwd, cols[i, j], preferred_element_type=F32) + bias
            pre[i, j] = act
            slope = 0.2 + 0.8 * jax.nn.sigmoid(act)
            grad[1 + i, 1 + j] = (ups[i // 2][j // 2] * slope).astype(BF16)
    kacc = jnp.zeros((128, 128), F32)
    for i in range(4):
        for j in range(0, 4, 2):
            pair = jnp.concatenate([grad[1 + i, 1 + j], grad[1 + i, 2 + j]], axis=1)
            for q in range(4):
                left = jnp.concatenate([cols[i, j, 128 * q:128 * q + 128, :],
                                        cols[i, j + 1, 128 * q:128 * q + 128, :]], axis=1)
                blocks = [jnp.zeros((32, 256), BF16)] * 4
                blocks[q] = pair
                kacc = kacc + nt_dot(left, jnp.concatenate(blocks, axis=0))
    terms[...] = kacc.reshape(16, 8, 128)

    per = 16 // n_one
    own = pl.ds(me_one * per, per)

    def copy_to(stage, device, src, dst):
        return pltpu.make_async_remote_copy(
            src_ref=src, dst_ref=dst, send_sem=stage_send.at[stage], recv_sem=stage_recv.at[stage],
            device_id=device, device_id_type=MESH)

    def shards(stage, number):
        ref = terms.at[pl.ds(0, number * per)] if number * per <= 16 else from_three.at[pl.ds(0, number)]
        return copy_to(stage, (blk, chn), ref, ref)

    def total(buf, n):
        acc = buf[0]
        for k in range(1, n):
            acc = acc + buf[k]
        return acc

    for k in far_first(n_one):
        other = lax.rem(me_one + k, n_one)
        copy_to(0, dev_one(other), terms.at[pl.ds(other * per, per)], from_one.at[me_one]).start()
    from_one[me_one] = terms[own]
    halo_start(grad, grad_send, grad_recv)
    halo_send_wait(wide, halo_send, halo_recv)

    shards(0, n_one - 1).wait_recv()
    from_two[me_two] = total(from_one, n_one)
    for r in range(n_two):
        @pl.when(me_two != r)
        def _(r=r):
            copy_to(2, dev_two(r), from_two.at[me_two], from_two.at[me_two]).start()

    pool_row = lax.broadcasted_iota(jnp.int32, (128, 64), 0)
    pool_lane = lax.broadcasted_iota(jnp.int32, (128, 64), 1)
    pool_map = jnp.where(lax.shift_right_logical(pool_row, 1) == pool_lane, 0.125, 0.0).astype(F32)
    def smooth_row(i, carry):
        v = pre[i]
        pre[i] = 0.2 * v + 0.8 * (jnp.maximum(v, 0.0) + jnp.log1p(jnp.exp(-jnp.abs(v))))
        return carry

    lax.fori_loop(0, 4, smooth_row, 0)
    sums = jnp.concatenate([pre[2 * i, 2 * j] + pre[2 * i, 2 * j + 1] + pre[2 * i + 1, 2 * j] + pre[2 * i + 1, 2 * j + 1]
                            for i in range(2) for j in range(2)], axis=0)
    means = jnp.dot(sums, pool_map, precision=lax.Precision.HIGHEST, preferred_element_type=F32)
    for i in range(2):
        for j in range(2):
            pool_f[:, i, j, :] = means[64 * i + 32 * j:64 * i + 32 * j + 32]
    pooled_o[...] = pool_f[...].astype(BF16)
    shards(0, n_one - 1).wait_send()

    shards(2, n_two - 1).wait_recv()
    from_three[me_three] = total(from_two, n_two)
    for root in range(2):
        @pl.when(me_three != root)
        def _(root=root):
            copy_to(1, dev_three(root), from_three.at[me_three], from_three.at[me_three]).start()
    shards(2, n_two - 1).wait_send()

    halo_recv_wait(grad, grad_send, grad_recv)
    for a in range(3):
        for b in range(3):
            t = 3 * a + b
            cols_back[:, :, 32 * t:32 * t + 32, :] = grad[a:a + 4, b:b + 4]
    zlane = lax.broadcasted_iota(jnp.int32, (16, 128), 1)
    def back_row(i, carry):
        for j in range(4):
            part = jnp.dot(w_back[...], cols_back[i, j], preferred_element_type=F32)
            before = jnp.where(zlane == 0, 0.0, pltpu.roll(part[:16], 1, 1))
            after = jnp.where(zlane == 127, 0.0, pltpu.roll(part[32:], 127, 1))
            vol_f[:, i, j, :] = before + part[16:32] + after
        return carry

    lax.fori_loop(0, 4, back_row, 0)
    vgrad_o[...] = vol_f[...].astype(BF16)
    halo_send_wait(grad, grad_send, grad_recv)

    @pl.when(is_root)
    def _():
        shards(1, 1).wait_send()
        shards(1, n_three - 1).wait_recv()
        result[own] = total(from_three, n_three)

    @pl.when(jnp.logical_not(is_root))
    def _():
        shards(1, 2).wait_send()
        shards(4, 1).wait_recv()

    for k in far_first(n_one):
        copy_to(3, dev_one(lax.rem(me_one + k, n_one)), result.at[own], result.at[own]).start()

    @pl.when(is_root)
    def _():
        for k in range(half):
            copy_to(4, dev_three(first_served + k), result.at[own], result.at[own]).start()

    shards(3, n_one - 1).wait_recv()
    full = result[...].reshape(128, 128)
    for q in range(4):
        part = full if q == 0 else pltpu.roll(full, 128 - 32 * q, 1)
        taps = 8 if q < 3 else 3
        kgrad_o[8 * q:8 * q + taps] = part[:16 * taps, :32].reshape(taps, 16, 32)
    bgrad_o[...] = part[48:49, :32]
    shards(3, n_one - 1).wait_send()

    @pl.when(is_root)
    def _():
        shards(4, half).wait_send()


def leave(pooled_v, vgrad_v, kgrad_v, bgrad_v, pooled_h, vgrad_h, kgrad_h, bgrad_h, sem):
    copies = [pltpu.make_async_copy(src, dst, sem.at[i]) for i, (src, dst) in enumerate(
        ((vgrad_v, vgrad_h), (kgrad_v, kgrad_h), (pooled_v, pooled_h), (bgrad_v, bgrad_h)))]
    for c in copies:
        c.start()
    for c in copies:
        c.wait()


def factors_of(mesh):
    nblock, nchan = mesh.shape["block"], mesh.shape["chan"]
    if (nblock, nchan) == (48, 16):
        return (8, 6, 4, 2, 2)
    return (2, nblock // 2, nchan // 4, 2, 2)


def local(factors, volume, weights, conv_bias, pooled_grad):
    ny, nzl, nx, nzh, ncore = factors
    n_one, n_two, n_three = nx * ncore, ny, nzh * nzl
    per = 16 // n_one
    vmem = pl.BlockSpec(memory_space=pltpu.VMEM)
    hbm = pl.BlockSpec(memory_space=pltpu.HBM)
    dma = pltpu.SemaphoreType.DMA
    shapes = (jax.ShapeDtypeStruct((32, 2, 2, 64), BF16), jax.ShapeDtypeStruct((16, 4, 4, 128), BF16),
              jax.ShapeDtypeStruct((27, 16, 32), F32), jax.ShapeDtypeStruct((1, 32), F32))
    outs = pl.pallas_call(
        functools.partial(kernel, factors),
        out_shape=shapes,
        in_specs=[hbm] * 4,
        out_specs=(vmem,) * 4,
        scratch_shapes=[
            pltpu.VMEM((16, 4, 4, 128), BF16),
            pltpu.VMEM((27, 16, 32), BF16),
            pltpu.VMEM((1, 32), F32),
            pltpu.VMEM((32, 2, 2, 64), BF16),
            pltpu.VMEM((16, 4, 4, 128), F32),
            pltpu.VMEM((32, 2, 2, 64), F32),
            pltpu.VMEM((32, 2, 2, 64), F32),
            pltpu.VMEM((6, 6, 16, 128), BF16),
            pltpu.VMEM((2, 6, 6, 16, 128), BF16),
            pltpu.VMEM((4, 4, 512, 128), BF16),
            pltpu.VMEM((4, 4, 32, 128), F32),
            pltpu.VMEM((6, 6, 32, 128), BF16),
            pltpu.VMEM((4, 4, 288, 128), BF16),
            pltpu.VMEM((48, 288), BF16),
            pltpu.VMEM((16, 8, 128), F32),
            pltpu.VMEM((n_one, per, 8, 128), F32),
            pltpu.VMEM((n_two, per, 8, 128), F32),
            pltpu.VMEM((n_three, per, 8, 128), F32),
            pltpu.VMEM((16, 8, 128), F32),
            dma((4,)), dma((8,)), dma((8,)), dma((8,)), dma((8,)), dma((5,)), dma((5,)),
        ],
        compiler_params=pltpu.CompilerParams(
            collective_id=0, has_side_effects=True, vmem_limit_bytes=32 * 1024 * 1024),
        name="conv_step",
    )(*[pltpu.with_memory_space_constraint(v, pltpu.HBM)
        for v in (volume, weights.transpose(1, 2, 0), conv_bias.reshape(1, 32), pooled_grad)])
    pooled, vgrad, kgrad, bgrad = pl.pallas_call(
        leave,
        out_shape=shapes,
        in_specs=[vmem] * 4,
        out_specs=(pl.BlockSpec(memory_space=pltpu.HBM),) * 4,
        scratch_shapes=[dma((4,))],
        compiler_params=pltpu.CompilerParams(vmem_limit_bytes=1024 * 1024),
        name="leave",
    )(*outs)
    return (pooled, vgrad, kgrad.transpose(2, 0, 1), bgrad.reshape(32))


def solution(mesh):
    placed = (P(None, "block", "chan", None), P(), P(), P(None, "block", "chan", None))
    return jax.shard_map(
        functools.partial(local, factors_of(mesh)),
        mesh=mesh,
        in_specs=placed,
        out_specs=(P(None, "block", "chan", None), P(None, "block", "chan", None), P(), P()),
        check_vma=False,
    )
```
